256 devices in a mesh: dp: 64 (over z, y, core), tp: 4 (over x).
Axes of the slice: x: 4, y: 4, z: 8, core: 2. Of those that a mesh axis runs over, the one named last changes fastest.
Arguments:
- attn_partial: bfloat16 [4, 4096, 7168], P('tp', 'dp'), may hold values from -3 to 3
- hidden_in: bfloat16 [4096, 7168], P('dp', 'tp'), may hold values from -6 to 6
- norm_gain: float32 [7168], replicated, may hold values from 0.5 to 1.5
- expert_ids: int32 [4096, 8], P('dp'), may hold values from 0 to 255, all different within a row; in each aligned block of 64 rows (0 to 63, 64 to 127, ...) at most 4 rows name the same one
- route_prob: bfloat16 [4096, 8], P('dp'), may hold values from 0.049804688 to 0.3984375
- w_gate: bfloat16 [64, 7168, 1024], P('dp', None, 'tp'), may hold values from -0.0625 to 0.0625
- w_up: bfloat16 [64, 7168, 1024], P('dp', None, 'tp'), may hold values from -0.0625 to 0.0625
- w_down: bfloat16 [64, 1024, 7168], P('dp', 'tp'), may hold values from -0.1875 to 0.1875
Outputs:
- layer_out: bfloat16 [4096, 7168], P('dp', 'tp')
- amax_input: float32 [64], P('dp')
- amax_hidden: float32 [64], P('dp')
The draws below stay inside these ranges and needn't reach their ends.
Inputs may be any that keep to these rules, and one draw needn't show every extreme that they name: `expert_ids`: each token names 8 different experts; within each aligned block of 64 tokens no expert is named by more than 4 tokens.
All inputs are finite; a program needn't handle non-finite values.
Results may differ from the reference program's by a relative error of at most 0.0075.
Values may be sent and summed in bfloat16 or wider, within the bound.
A program may use at most 64 MiB of HBM per device.

```python
import math
import jax
import jax.numpy as jnp
import numpy as np
from jax import lax

MODEL_WIDTH = 7168
ROUTED = 256
TOP = 8
FF = 1024
TOK_DEV = 64
TOKENS = 4096
GROUPS = 4
EXPERTS = 64
EXPERT_SLOTS = 4
N_DP = 64


def shard_levels(stream_key, shape, shards, smallest, high):
    level = 1.0
    for axis_at, shards_of in shards:
        heights = jax.random.uniform(jax.random.fold_in(jax.random.fold_in(stream_key, 6), axis_at), (shards_of,), jnp.float32, smallest / len(shards), high / len(shards))
        level = level * jnp.repeat(jnp.exp(heights), shape[axis_at] // shards_of).reshape((-1,) + (1,) * (len(shape) - 1 - axis_at))
    return level


def shared_out(own_key, own, number, rows, number_of, top, most, skew):
    sequence = jax.random.permutation(own_key, number_of)
    crowded, common = portions_of(number_of, rows * top, most, skew, True), portions_of(number_of, rows * top, most, skew, False)
    places = jnp.arange(number_of)

    def named(tallies, offset_by):
        used = int((tallies > 0).sum())
        fixed = max(1, used // 4)
        shifted = fixed + (places - fixed + offset_by * (used - fixed)) % max(1, number_of - fixed)
        return jnp.zeros((number_of,), jnp.int32).at[sequence[jnp.where(places < fixed, places, shifted)]].set(jnp.asarray(tallies, jnp.int32))

    tallies = jnp.where(number % 4 == 0, named(crowded, number // 4), named(common, number - number // 4 - 1))
    mixed = jax.random.permutation(jax.random.fold_in(own, 3), number_of)
    giver, sink = mixed[0:number_of // 2 * 2:2], mixed[1:number_of // 2 * 2:2]
    room = jnp.minimum(tallies[giver] - 1, most - tallies[sink]) // 2
    room = jnp.where((giver == sequence[0]) | (sink == sequence[0]) | (tallies[sink] == 0), 0, jnp.maximum(room, 0))
    shifted = jax.random.randint(jax.random.fold_in(own, 4), (number_of // 2,), 0, 1 << 20) % (room + 1)
    tallies = tallies.at[giver].add(-shifted).at[sink].add(shifted)
    items = jnp.searchsorted(jnp.cumsum(tallies), jnp.arange(rows * top), side="right").astype(jnp.int32)
    table = items.reshape(top, rows).T
    table = table[jax.random.permutation(jax.random.fold_in(own, 1), rows)]
    offset_by = jax.random.randint(jax.random.fold_in(own, 2), (rows, 1), 0, top)
    return jnp.take_along_axis(table, (jnp.arange(top)[None, :] + offset_by) % top, axis=1)


def portions_of(amount, total, bound, skew, full):
    portions = [(1 << 20) // math.isqrt(grade ** skew) + 1 for grade in range(1, amount + 1)]
    largest = bound if full else min(bound, max(-(-total // amount), total * portions[0] // sum(portions)))
    least = 1 if total - largest >= amount - 1 else 0
    counts, spare = [largest] + [least] * (amount - 1), total - largest - least * (amount - 1)
    while spare > 0:
        movable = [i for i in range(1, amount) if counts[i] < largest] or [i for i in range(1, amount) if counts[i] < bound]
        mass, budget = sum([portions[i] for i in movable]), spare
        for i in movable:
            extra = min(bound - counts[i], max(1, budget * portions[i] // mass), spare)
            counts[i] = counts[i] + extra
            spare = spare - extra
    return np.array(counts)


def gaussian(own_key, extent, spread, bound, cuts=(), kind=jnp.bfloat16):
    result = spread * jax.random.normal(own_key, extent, jnp.float32)
    if cuts:
        result = result * shard_levels(own_key, extent, cuts, -0.22, 0.18)
    return jnp.clip(result, -bound, bound).astype(kind)


def setup_inputs(seed: int = 0) -> dict:
    keys = jax.random.split(jax.random.key(seed), 9)
    attn_partial = gaussian(keys[0], (GROUPS, TOKENS, MODEL_WIDTH), 0.5, 3.0, ((0, 4), (1, 64)))
    hidden_in = gaussian(keys[1], (TOKENS, MODEL_WIDTH), 1.0, 6.0, ((0, 64), (1, 4)))
    norm_gain = jnp.clip(1.0 + 0.1 * jax.random.normal(keys[2], (MODEL_WIDTH,), jnp.float32), 0.5, 1.5)
    expert_ids_keys = jax.random.split(jax.random.fold_in(keys[3], 1), TOKENS // TOK_DEV)
    expert_ids_turns = jax.random.permutation(jax.random.fold_in(keys[3], 3), TOKENS // TOK_DEV)
    expert_ids = jax.vmap(lambda own, number: shared_out(jax.random.fold_in(keys[3], 2), own, number, TOK_DEV, ROUTED, TOP, EXPERT_SLOTS, 2))(expert_ids_keys, expert_ids_turns).reshape((TOKENS, TOP))
    route_prob = jnp.clip(0.049804688 + 0.3486328 * jax.random.uniform(keys[4], (TOKENS, TOP), jnp.float32) ** shard_levels(keys[4], (TOKENS, TOP), ((0, 64),), -0.2, 0.2), 0.049804688, 0.3984375).astype(jnp.bfloat16)
    w_gate = gaussian(keys[5], (EXPERTS, MODEL_WIDTH, FF), MODEL_WIDTH ** -0.5, 0.0625, ((0, 64), (2, 4)))
    w_up = gaussian(keys[6], (EXPERTS, MODEL_WIDTH, FF), MODEL_WIDTH ** -0.5, 0.0625, ((0, 64), (2, 4)))
    w_down = gaussian(keys[7], (EXPERTS, FF, MODEL_WIDTH), FF ** -0.5, 0.1875, ((0, 64), (1, 4)))
    return {"attn_partial": attn_partial, "hidden_in": hidden_in, "norm_gain": norm_gain, "expert_ids": expert_ids, "route_prob": route_prob, "w_gate": w_gate, "w_up": w_up, "w_down": w_down}


eps = 1e-06

def route_tables(ids_block, prob_block, experts, capacity):
    matches = ids_block[:, :, None] == jnp.arange(experts, dtype=jnp.int32)[None, None, :]
    onehot = lax.optimization_barrier(jnp.sum(matches.astype(jnp.int32), axis=1))
    weight = lax.optimization_barrier(jnp.sum(jnp.where(matches, prob_block[:, :, None].astype(jnp.float32), jnp.float32(0.0)), axis=1))
    before = jnp.cumsum(onehot, axis=0) - onehot
    placing = (onehot.T[:, None, :] == 1) & (before.T[:, None, :] == jnp.arange(capacity, dtype=jnp.int32)[None, :, None])
    return (placing, weight)

def reference(attn_partial, hidden_in, norm_gain, expert_ids, route_prob, w_gate, w_up, w_down):
    experts = N_DP
    residual = hidden_in.astype(jnp.float32) + lax.optimization_barrier(jnp.sum(attn_partial.astype(jnp.float32), axis=0))
    mean_sq = lax.optimization_barrier(jnp.mean(residual * residual, axis=1, keepdims=True))
    normed = (residual * lax.rsqrt(mean_sq + eps) * norm_gain).astype(jnp.bfloat16)
    ids_blocks = expert_ids.reshape(N_DP, TOK_DEV, TOP)
    probability_blocks = route_prob.reshape(N_DP, TOK_DEV, TOP)
    normalized_blocks = normed.reshape(N_DP, TOK_DEV, MODEL_WIDTH).astype(jnp.float32)
    placing, weight = jax.vmap(lambda ids_block, prob_block: route_tables(ids_block, prob_block, experts, EXPERT_SLOTS))(ids_blocks, probability_blocks)

    def expert(operands):
        selection_mask, gate_w, up_w, down_w = operands
        expert_slot_rows = jnp.einsum('jrn,jnf->jrf', selection_mask.astype(jnp.float32), normalized_blocks).astype(jnp.bfloat16).reshape(N_DP * EXPERT_SLOTS, MODEL_WIDTH)
        gate_val = jnp.dot(expert_slot_rows, gate_w, preferred_element_type=jnp.float32)
        up_val = jnp.dot(expert_slot_rows, up_w, preferred_element_type=jnp.float32)
        hidden_act = (jax.nn.silu(gate_val) * up_val).astype(jnp.bfloat16)
        expert_out = jnp.dot(hidden_act, down_w, preferred_element_type=jnp.float32)
        input_peak = jnp.max(jnp.abs(expert_slot_rows.astype(jnp.float32)))
        hidden_peak = jnp.max(jnp.abs(hidden_act.astype(jnp.float32)))
        return (expert_out.reshape(N_DP, EXPERT_SLOTS, MODEL_WIDTH), input_peak, hidden_peak)
    expert_outs, amax_input, amax_hidden = lax.map(expert, (jnp.swapaxes(placing, 0, 1), w_gate, w_up, w_down))

    def combine(operands):
        selection_mask, block_weight, returned = operands
        combine_matrix = (selection_mask.astype(jnp.float32) * block_weight.T[:, None, :]).reshape(experts * EXPERT_SLOTS, TOK_DEV)
        return jnp.dot(combine_matrix.T, returned.reshape(experts * EXPERT_SLOTS, MODEL_WIDTH), precision=lax.Precision.HIGHEST, preferred_element_type=jnp.float32)
    moe_out = lax.map(combine, (placing, weight, jnp.swapaxes(expert_outs, 0, 1)))
    layer_out = (residual + moe_out.reshape(TOKENS, MODEL_WIDTH)).astype(jnp.bfloat16)
    return (layer_out, amax_input, amax_hidden)
```

```python
import jax
import jax.numpy as jnp
from jax import lax
from jax.sharding import PartitionSpec as P

SLOTS = 4
eps = 1e-06


def on_device(attn_partial, hidden_in, norm_gain, expert_ids, route_prob, w_gate, w_up, w_down):
    experts = lax.axis_size("dp")
    tps = lax.axis_size("tp")
    tp_index = lax.axis_index("tp")
    tokens, columns = hidden_in.shape
    width = tps * columns
    pieces = jnp.swapaxes(attn_partial[0].reshape(tokens, tps, columns), 0, 1)
    pieces = lax.all_to_all(pieces, "tp", split_axis=0, concat_axis=0, tiled=True)
    residual = hidden_in.astype(jnp.float32) + jnp.sum(pieces.astype(jnp.float32), axis=0)
    square = lax.psum(jnp.sum(residual * residual, axis=1, keepdims=True), "tp")
    gain = lax.dynamic_slice_in_dim(norm_gain, tp_index * columns, columns, 0)
    normed = (residual * lax.rsqrt(square / width + eps) * gain).astype(jnp.bfloat16)

    matches = expert_ids[:, :, None] == jnp.arange(experts, dtype=jnp.int32)[None, None, :]
    named = jnp.any(matches, axis=1)
    weight = jnp.sum(jnp.where(matches, route_prob[:, :, None].astype(jnp.float32), 0.0), axis=1)
    earlier = jnp.tri(tokens, tokens, -1, dtype=jnp.bfloat16)
    before = jnp.dot(earlier, named.astype(jnp.bfloat16), preferred_element_type=jnp.float32)
    slot = jnp.arange(SLOTS, dtype=jnp.float32)[None, :, None]
    placing = named.T[:, None, :] & (before.T[:, None, :] == slot)
    selection = placing.reshape(experts * SLOTS, tokens).astype(jnp.bfloat16)
    combine = (placing.astype(jnp.float32) * weight.T[:, None, :]).reshape(experts * SLOTS, tokens)

    outgoing = jnp.dot(selection, normed, preferred_element_type=jnp.float32).astype(jnp.bfloat16)
    rows = lax.all_to_all(
        outgoing.reshape(experts, SLOTS, columns), "dp", split_axis=0, concat_axis=0, tiled=True
    ).reshape(experts * SLOTS, columns)
    rows = lax.all_gather(rows, "tp", axis=0, tiled=False)
    gate = sum(jnp.dot(rows[i], w_gate[0][i * columns:(i + 1) * columns], preferred_element_type=jnp.float32) for i in range(tps))
    up = sum(jnp.dot(rows[i], w_up[0][i * columns:(i + 1) * columns], preferred_element_type=jnp.float32) for i in range(tps))
    act = (jax.nn.silu(gate) * up).astype(jnp.bfloat16)
    partial = jnp.dot(act, w_down[0], preferred_element_type=jnp.float32).astype(jnp.bfloat16)
    amax_input = jnp.max(jnp.abs(rows)).astype(jnp.float32).reshape(1)
    amax_hidden = lax.pmax(jnp.max(jnp.abs(act)).astype(jnp.float32).reshape(1), "tp")
    out = lax.psum_scatter(partial, "tp", scatter_dimension=1, tiled=True)
    back = lax.all_to_all(
        out.reshape(experts, SLOTS, columns), "dp", split_axis=0, concat_axis=0, tiled=True
    ).reshape(experts * SLOTS, columns)
    moe = jnp.dot(combine.T, back.astype(jnp.float32), precision=lax.Precision.HIGHEST, preferred_element_type=jnp.float32)
    return (residual + moe).astype(jnp.bfloat16), amax_input, amax_hidden


def solution(mesh):
    placed = (
        P("tp", "dp", None),
        P("dp", "tp"),
        P(),
        P("dp", None),
        P("dp", None),
        P("dp", None, "tp"),
        P("dp", None, "tp"),
        P("dp", "tp", None),
    )
    return jax.shard_map(
        on_device,
        mesh=mesh,
        in_specs=placed,
        out_specs=(P("dp", "tp"), P("dp"), P("dp")),
        check_vma=False,
    )
```

```python
import jax
import jax.numpy as jnp
from jax import lax
from jax.experimental import pallas as pl
from jax.experimental.pallas import tpu as pltpu
from jax.sharding import PartitionSpec as P

MESH = pl.DeviceIdType.MESH
SLOTS = 4
EPS = 1e-06
NZ, NY, TPS = 8, 4, 4
CHIPS = NZ * NY
BLOCK = 2 * SLOTS
ROWS = CHIPS * BLOCK
CHUNKS = 4
PER = CHIPS // CHUNKS
CROWS = ROWS // CHUNKS
HALF = CROWS // 2
F32, BF16 = jnp.float32, jnp.bfloat16


def body(
    ids, prob, attn, hidden, gain, wg, wu, wd,
    out, amax_in, amax_hid,
    hid_v, gain_v, wg_v, wu_v, wd_v, local_sem,
    route, route_sem,
    ar, af, a_send, a_recv,
    res, sq, sq_send, sq_recv,
    nb, nb_sem, select, combine,
    og, rows, d_send, d_recv,
    g_send, g_recv,
    act, own, pb, rf, rs, fs, r_send, r_recv,
    oq, back, b_send, b_recv,
    mo, mr, m_sem,
    hm, h_send, h_recv, peak,
):
    me, t = lax.axis_index("dp"), lax.axis_index("tp")
    c, chip = lax.rem(me, 2), lax.div(me, 2)
    z, y = lax.div(chip, NY), lax.rem(chip, NY)
    tokens, width = attn.shape
    cols = width // TPS
    right, left, far = lax.rem(t + 1, TPS), lax.rem(t + 3, TPS), lax.rem(t + 2, TPS)
    mate = chip * 2 + 1 - c

    def step_of(d):
        m, dy = lax.div(d, NY), lax.rem(d, NY)
        odd = lax.rem(m, 2)
        dz = odd * lax.div(m + 1, 2) + (1 - odd) * lax.rem(NZ - lax.div(m, 2), NZ)
        return dz, dy

    def ahead(d):
        dz, dy = step_of(d)
        return (lax.rem(z + dz, NZ) * NY + lax.rem(y + dy, NY)) * 2 + c

    def behind(d):
        dz, dy = step_of(d)
        return (lax.rem(z + NZ - dz, NZ) * NY + lax.rem(y + NY - dy, NY)) * 2 + c

    def remote(src, dst, ssem, rsem, dp, tp):
        return pltpu.make_async_remote_copy(
            src_ref=src, dst_ref=dst, send_sem=ssem, recv_sem=rsem,
            device_id=(dp, tp), device_id_type=MESH,
        )

    def quarter(q):
        return pl.ds(pl.multiple_of(q * cols, 128), cols)

    def block(d):
        return pl.ds(pl.multiple_of(d * BLOCK, BLOCK), BLOCK)

    barrier = pltpu.get_barrier_semaphore()

    def greet(d, carry):
        pl.semaphore_signal(barrier, inc=1, device_id=(ahead(d), t), device_id_type=MESH)
        return carry

    for r in range(1, TPS):
        pl.semaphore_signal(barrier, inc=1, device_id=(me, lax.rem(t + r, TPS)), device_id_type=MESH)
    pl.semaphore_signal(barrier, inc=1, device_id=(mate, t), device_id_type=MESH)
    lax.fori_loop(1, CHIPS, greet, 0)

    loads = [
        pltpu.make_async_copy(attn.at[:, quarter(t)], ar.at[3], local_sem.at[0]),
        pltpu.make_async_copy(hidden, hid_v, local_sem.at[1]),
        pltpu.make_async_copy(gain.at[:, quarter(t)], gain_v, local_sem.at[2]),
        pltpu.make_async_copy(wg, wg_v, local_sem.at[3]),
        pltpu.make_async_copy(wu, wu_v, local_sem.at[4]),
        pltpu.make_async_copy(wd, wd_v, local_sem.at[5]),
    ]
    for load in loads:
        load.start()

    lane = lax.broadcasted_iota(jnp.int32, (8, 128), 1)
    mine = (lane >> 6) == c
    idf, prf = ids[...].astype(F32), prob[...].astype(F32)
    route[c, 0:8, :] = jnp.where(mine, jnp.concatenate([idf, idf], axis=1), 0.0)
    route[c, 8:16, :] = jnp.where(mine, jnp.concatenate([prf, prf], axis=1), 0.0)

    pl.semaphore_wait(barrier, CHIPS - 1 + 1 + TPS - 1)

    h = tokens // 2
    exchange = [
        remote(attn.at[0:h, quarter(far)], af.at[0], a_send.at[0], a_recv.at[0], me, right),
        remote(attn.at[h:tokens, quarter(far)], af.at[1], a_send.at[1], a_recv.at[1], me, left),
        remote(attn.at[:, quarter(right)], ar.at[0], a_send.at[2], a_recv.at[2], me, right),
        remote(attn.at[:, quarter(left)], ar.at[1], a_send.at[3], a_recv.at[3], me, left),
    ]
    for e in exchange:
        e.start()
    routes = remote(route.at[c], route.at[c], route_sem.at[0], route_sem.at[1], mate, t)
    routes.start()
    onward = [
        remote(af.at[0], ar.at[2, 0:h], a_send.at[4], a_recv.at[4], me, right),
        remote(af.at[1], ar.at[2, h:tokens], a_send.at[5], a_recv.at[5], me, left),
    ]
    for i in range(2):
        exchange[i].wait_recv()
        onward[i].start()

    routes.wait_recv()
    both = route[0] + route[1]
    j = lax.broadcasted_iota(jnp.int32, (ROWS, 128), 0)
    tok = lax.broadcasted_iota(jnp.int32, (ROWS, 128), 1)
    d, slot = j >> 3, j & 3
    m, dy = d >> 2, d & 3
    dz = jnp.where((m & 1) == 1, (m + 1) >> 1, (NZ - (m >> 1)) & (NZ - 1))
    expert = ((((z + dz) & (NZ - 1)) * NY + ((y + dy) & (NY - 1))) * 2 + c).astype(F32)
    weight = jnp.zeros((ROWS, 128), F32)
    match = jnp.zeros((ROWS, 128), F32)
    for k in range(8):
        hit = both[k:k + 1, :] == expert
        match = jnp.where(hit, 1.0, match)
        weight = jnp.where(hit, both[8 + k:9 + k, :], weight)
    a, b = lax.broadcasted_iota(jnp.int32, (128, 128), 0), lax.broadcasted_iota(jnp.int32, (128, 128), 1)
    earlier = jnp.where((a < b) & ((a >> 6) == (b >> 6)), 1.0, 0.0).astype(BF16)
    before = jnp.dot(match.astype(BF16), earlier, preferred_element_type=F32)
    placed = jnp.where((before == slot.astype(F32)) & (((j >> 2) & 1) == (tok >> 6)), match, 0.0)
    select[...] = placed.astype(BF16)
    combine[...] = jnp.transpose(placed * weight).astype(BF16)

    for i in range(3):
        loads[i].wait()
    exchange[2].wait_recv()
    exchange[3].wait_recv()
    onward[0].wait_recv()
    onward[1].wait_recv()
    tile = 256
    squares = jnp.zeros((tokens, tile), F32)
    for i in range(cols // tile):
        s = slice(i * tile, (i + 1) * tile)
        v = hid_v[:, s].astype(F32)
        for q in range(4):
            v = v + ar[q, :, s].astype(F32)
        res[:, s] = v
        squares = squares + v * v
    sq[0] = jnp.broadcast_to(jnp.sum(squares, axis=1, keepdims=True), (tokens, 128))
    share = [
        remote(sq.at[0], sq.at[r], sq_send.at[r - 1], sq_recv.at[r - 1], me, lax.rem(t + r, TPS))
        for r in range(1, TPS)
    ]
    for s in share:
        s.start()
    for s in share:
        s.wait_recv()
    inv = lax.rsqrt((sq[0] + sq[1] + sq[2] + sq[3]) / width + EPS)
    here = pl.ds(pl.multiple_of(c * tokens, tokens), tokens)
    there = pl.ds(pl.multiple_of((1 - c) * tokens, tokens), tokens)
    for i in range(cols // 128):
        s = slice(i * 128, (i + 1) * 128)
        nb[here, s] = (res[:, s] * inv * gain_v[:, s]).astype(BF16)
    swap = remote(nb.at[here], nb.at[here], nb_sem.at[0], nb_sem.at[1], mate, t)
    swap.start()
    swap.wait_recv()

    def outward(d):
        return remote(og.at[block(d)], rows.at[0, block(d)], d_send.at[d], d_recv.at[d], ahead(d), t)

    keep = pltpu.make_async_copy(og.at[0:BLOCK], rows.at[0, 0:BLOCK], d_recv.at[0])

    def go(d, carry):
        outward(d).start()
        return carry

    for k in range(CHUNKS):
        r = slice(k * CROWS, (k + 1) * CROWS)
        og[r, :] = jnp.dot(select[r, :], nb[...], preferred_element_type=F32).astype(BF16)
        if k == 0:
            keep.start()
        lax.fori_loop(max(1, k * PER), (k + 1) * PER, go, 0)

    def arrive(d, carry):
        outward(d).wait_recv()
        return carry

    def gather(k):
        r = slice(k * CROWS, (k + 1) * CROWS)
        lo, hi = slice(k * CROWS, k * CROWS + HALF), slice(k * CROWS + HALF, (k + 1) * CROWS)
        return [
            remote(rows.at[0, r], rows.at[1, r], g_send.at[k, 0], g_recv.at[k, 0], me, right),
            remote(rows.at[0, r], rows.at[3, r], g_send.at[k, 1], g_recv.at[k, 1], me, left),
            remote(rows.at[1, lo], rows.at[2, lo], g_send.at[k, 2], g_recv.at[k, 2], me, right),
            remote(rows.at[3, hi], rows.at[2, hi], g_send.at[k, 3], g_recv.at[k, 3], me, left),
        ]

    gathers = [gather(k) for k in range(CHUNKS)]

    def fetch(k):
        if k == 0:
            keep.wait()
        lax.fori_loop(max(1, k * PER), (k + 1) * PER, arrive, 0)
        gathers[k][0].start()
        gathers[k][1].start()

    def pass_on(k):
        gathers[k][0].wait_recv()
        gathers[k][2].start()
        gathers[k][1].wait_recv()
        gathers[k][3].start()

    def row_peak(k):
        r = slice(k * CROWS, (k + 1) * CROWS)
        top = peak[0]
        for q in range(4):
            for i in range(cols // 256):
                v = jnp.abs(rows[q, r, i * 256:(i + 1) * 256].astype(F32))
                top = jnp.maximum(top, jnp.max(v.reshape(CROWS // 8, 8, 256), axis=0))
        peak[0] = top

    def hidden_rows(k):
        r = slice(k * CROWS, (k + 1) * CROWS)
        g = jnp.zeros((CROWS, wg_v.shape[1]), F32)
        u = jnp.zeros((CROWS, wu_v.shape[1]), F32)
        for q, src in ((0, t), (1, left), (2, far), (3, right)):
            w = pl.ds(pl.multiple_of(src * cols, 256), cols)
            x = rows[q, r, :]
            g = g + jnp.dot(x, wg_v[w, :], preferred_element_type=F32)
            u = u + jnp.dot(x, wu_v[w, :], preferred_element_type=F32)
        v = (g / (1.0 + jnp.exp(-g)) * u).astype(BF16)
        act[r, :] = v
        v = jnp.abs(v.astype(F32))
        peak[1] = jnp.maximum(peak[1], jnp.max(v.reshape(CROWS // 8, 8, v.shape[1]), axis=0))

    def down(k):
        r = slice(k * CROWS, (k + 1) * CROWS)
        x = act[r, :]
        for i, dst in ((1, far), (0, right), (2, left)):
            pb[i, r, :] = jnp.dot(x, wd_v[:, quarter(dst)], preferred_element_type=F32).astype(BF16)
        own[r, :] = jnp.dot(x, wd_v[:, quarter(t)], preferred_element_type=F32)

    peak[...] = jnp.zeros(peak.shape, F32)

    def finish_gather(k):
        gathers[k][2].wait_recv()
        gathers[k][3].wait_recv()
        hidden_rows(k)
        down(k)

    def reduce(k):
        r0 = k * CROWS
        lo, hi = slice(r0, r0 + HALF), slice(r0 + HALF, r0 + CROWS)
        f = slice(k * HALF, (k + 1) * HALF)
        return [
            remote(pb.at[1, lo], rf.at[0, f], r_send.at[k, 0], r_recv.at[k, 0], me, right),
            remote(pb.at[1, hi], rf.at[1, f], r_send.at[k, 1], r_recv.at[k, 1], me, left),
            remote(pb.at[0, hi], rs.at[0, hi], r_send.at[k, 2], r_recv.at[k, 2], me, right),
            remote(pb.at[2, lo], rs.at[1, lo], r_send.at[k, 3], r_recv.at[k, 3], me, left),
            remote(fs.at[0, f], rs.at[0, lo], r_send.at[k, 4], r_recv.at[k, 4], me, right),
            remote(fs.at[1, f], rs.at[1, hi], r_send.at[k, 5], r_recv.at[k, 5], me, left),
        ]

    reduces = [reduce(k) for k in range(CHUNKS)]

    def first_hop(k):
        for i in range(4):
            reduces[k][i].start()

    def second_hop(k):
        r0 = k * CROWS
        f = slice(k * HALF, (k + 1) * HALF)
        reduces[k][0].wait_recv()
        fs[0, f] = (rf[0, f].astype(F32) + pb[0, r0:r0 + HALF].astype(F32)).astype(BF16)
        reduces[k][4].start()
        reduces[k][1].wait_recv()
        fs[1, f] = (rf[1, f].astype(F32) + pb[2, r0 + HALF:r0 + CROWS].astype(F32)).astype(BF16)
        reduces[k][5].start()

    def homeward(d):
        return remote(oq.at[block(d)], back.at[block(d)], b_send.at[d], b_recv.at[d], behind(d), t)

    stay = pltpu.make_async_copy(oq.at[0:BLOCK], back.at[0:BLOCK], b_recv.at[0])

    def go_home(d, carry):
        homeward(d).start()
        return carry

    def send_back(k):
        r = slice(k * CROWS, (k + 1) * CROWS)
        for i in range(2, 6):
            reduces[k][i].wait_recv()
        oq[r, :] = (own[r, :] + rs[0, r].astype(F32) + rs[1, r].astype(F32)).astype(BF16)
        if k == 0:
            stay.start()
        lax.fori_loop(max(1, k * PER), (k + 1) * PER, go_home, 0)

    for k in range(CHUNKS + 2):
        if k < CHUNKS:
            fetch(k)
        if 1 <= k <= CHUNKS:
            pass_on(k - 1)
        if k == 2:
            for load in loads[3:]:
                load.wait()
        if k >= 2:
            finish_gather(k - 2)

    order = (2, 3, 1, 0)
    for i in range(CHUNKS + 2):
        if i < CHUNKS:
            first_hop(order[i])
        if 1 <= i <= CHUNKS:
            second_hop(order[i - 1])
        if i >= 2:
            send_back(order[i - 2])
        if i == 0:
            for k in range(CHUNKS):
                row_peak(k)
            hm[0] = jnp.broadcast_to(jnp.max(peak[1]), (8, 128))
            tops = [
                remote(hm.at[0], hm.at[r], h_send.at[r - 1], h_recv.at[r - 1], me, lax.rem(t + r, TPS))
                for r in range(1, TPS)
            ]
            for s in tops:
                s.start()
            amax_in[0] = jnp.max(peak[0])

    def returned(d, carry):
        homeward(d).wait_recv()
        return carry

    for s in tops:
        s.wait_recv()
    amax_hid[0] = jnp.max(jnp.maximum(jnp.maximum(hm[0], hm[1]), jnp.maximum(hm[2], hm[3])))
    stay.wait()
    lax.fori_loop(1, CHIPS, returned, 0)
    mo[...] = jnp.dot(combine[there, :], back[...], preferred_element_type=F32)
    give = remote(mo, mr, m_sem.at[0], m_sem.at[1], mate, t)
    give.start()
    res[...] = res[...] + jnp.dot(combine[here, :], back[...], preferred_element_type=F32)
    give.wait_recv()
    out[...] = (res[...] + mr[...]).astype(BF16)

    for s in (*exchange, *onward, routes, *share, swap, *tops, give):
        s.wait_send()
    for k in range(CHUNKS):
        for s in (*gathers[k], *reduces[k]):
            s.wait_send()

    def drained(d, carry):
        outward(d).wait_send()
        homeward(d).wait_send()
        return carry

    lax.fori_loop(1, CHIPS, drained, 0)


def on_device(attn_partial, hidden_in, norm_gain, expert_ids, route_prob, w_gate, w_up, w_down):
    tokens, cols = hidden_in.shape
    width, ff = w_gate.shape[1:]
    vmem, anywhere = pl.BlockSpec(memory_space=pltpu.VMEM), pl.BlockSpec(memory_space=pl.ANY)
    smem = pl.BlockSpec(memory_space=pltpu.SMEM)
    dma = pltpu.SemaphoreType.DMA
    V = pltpu.VMEM
    scratch = [
        V((tokens, cols), BF16), V((1, cols), F32), V((width, ff), BF16), V((width, ff), BF16), V((ff, width), BF16), dma((6,)),
        V((2, 16, 128), F32), dma((2,)),
        V((4, tokens, cols), BF16), V((2, tokens // 2, cols), BF16), dma((6,)), dma((6,)),
        V((tokens, cols), F32), V((4, tokens, 128), F32), dma((3,)), dma((3,)),
        V((2 * tokens, cols), BF16), dma((2,)), V((ROWS, 128), BF16), V((128, ROWS), BF16),
        V((ROWS, cols), BF16), V((4, ROWS, cols), BF16), dma((CHIPS,)), dma((CHIPS,)),
        dma((CHUNKS, 4)), dma((CHUNKS, 4)),
        V((ROWS, ff), BF16), V((ROWS, cols), F32), V((3, ROWS, cols), BF16), V((2, ROWS // 2, cols), BF16),
        V((2, ROWS, cols), BF16), V((2, ROWS // 2, cols), BF16), dma((CHUNKS, 6)), dma((CHUNKS, 6)),
        V((ROWS, cols), BF16), V((ROWS, cols), BF16), dma((CHIPS,)), dma((CHIPS,)),
        V((tokens, cols), F32), V((tokens, cols), F32), dma((2,)),
        V((4, 8, 128), F32), dma((3,)), dma((3,)), V((2, 8, 256), F32),
    ]
    return pl.pallas_call(
        body,
        out_shape=(
            jax.ShapeDtypeStruct((tokens, cols), BF16),
            jax.ShapeDtypeStruct((1,), F32),
            jax.ShapeDtypeStruct((1,), F32),
        ),
        in_specs=[vmem, vmem] + [anywhere] * 6,
        out_specs=(vmem, smem, smem),
        scratch_shapes=scratch,
        compiler_params=pltpu.CompilerParams(
            collective_id=0, has_side_effects=True, vmem_limit_bytes=56 << 20
        ),
    )(
        expert_ids.T, route_prob.T, attn_partial[0], hidden_in, norm_gain[None],
        w_gate[0], w_up[0], w_down[0],
    )


def solution(mesh):
    placed = (
        P("tp", "dp", None),
        P("dp", "tp"),
        P(),
        P("dp", None),
        P("dp", None),
        P("dp", None, "tp"),
        P("dp", None, "tp"),
        P("dp", "tp", None),
    )
    return jax.shard_map(
        on_device,
        mesh=mesh,
        in_specs=placed,
        out_specs=(P("dp", "tp"), P("dp"), P("dp")),
        check_vma=False,
    )
```

```python
import jax
import jax.numpy as jnp
from jax import lax
from jax.experimental import pallas as pl
from jax.experimental.pallas import tpu as pltpu
from jax.sharding import PartitionSpec as P

MESH = pl.DeviceIdType.MESH
SLOTS = 4
EPS = 1e-06
NZ, NY, TPS = 8, 4, 4
CHIPS = NZ * NY
BLOCK = 2 * SLOTS
ROWS = CHIPS * BLOCK
CHUNKS = 4
PER = CHIPS // CHUNKS
CROWS = ROWS // CHUNKS
HALF = CROWS // 2
F32, BF16 = jnp.float32, jnp.bfloat16
PARTS = ((0, 768), (768, 1024))
EXTRA = 128
FIRST, LAST = (0, 1, 2, 3), (2, 3, 1, 0)


def body(
    ids, prob, attn, hidden, gain, wg, wu, wd,
    out, amax_in, amax_hid,
    hid_v, gain_v, wg_v, wu_v, wd_v, local_sem, known,
    route, route_sem,
    ar, af, a_send, a_recv,
    res, sq, sq_send, sq_recv,
    nb, nb_sem, select, combine,
    og, rows, d_send, d_recv, keep_sem,
    g_send, g_recv,
    g_acc, u_acc, act, own, pb, rf, rs, fs, r_send, r_recv,
    oq, back, b_send, b_recv,
    mo, mr, m_sem,
    hm, h_send, h_recv, peak,
):
    me, t = lax.axis_index("dp"), lax.axis_index("tp")
    c, chip = lax.rem(me, 2), lax.div(me, 2)
    z, y = lax.div(chip, NY), lax.rem(chip, NY)
    tokens, width = attn.shape
    cols = width // TPS
    right, left, far = lax.rem(t + 1, TPS), lax.rem(t + 3, TPS), lax.rem(t + 2, TPS)
    mate = chip * 2 + 1 - c

    def along_z(k):
        return (lax.rem(z + k, NZ) * NY + y) * 2 + c

    def along_y(k):
        return (z * NY + lax.rem(y + k, NY)) * 2 + c

    def remote(src, dst, ssem, rsem, dp, tp):
        return pltpu.make_async_remote_copy(
            src_ref=src, dst_ref=dst, send_sem=ssem, recv_sem=rsem,
            device_id=(dp, tp), device_id_type=MESH,
        )

    def tell(sem, dp, tp):
        pl.semaphore_signal(sem, inc=1, device_id=(dp, tp), device_id_type=MESH)

    def quarter(q, start=0, size=None):
        return pl.ds(pl.multiple_of(q * cols + start, 128), cols if size is None else size)

    def block(d):
        return pl.ds(pl.multiple_of(d * BLOCK, BLOCK), BLOCK)

    barrier = pltpu.get_barrier_semaphore()
    for r in range(1, TPS):
        tell(barrier, me, lax.rem(t + r, TPS))
    tell(barrier, mate, t)
    for k in (1, NZ - 1):
        tell(barrier, along_z(k), t)
    for k in (1, NY - 1):
        tell(barrier, along_y(k), t)

    loads = [
        pltpu.make_async_copy(attn.at[:, quarter(t)], ar.at[3], local_sem.at[0]),
        pltpu.make_async_copy(hidden, hid_v, local_sem.at[1]),
        pltpu.make_async_copy(gain.at[:, quarter(t)], gain_v, local_sem.at[2]),
        pltpu.make_async_copy(wg, wg_v, local_sem.at[3]),
        pltpu.make_async_copy(wu, wu_v, local_sem.at[4]),
        pltpu.make_async_copy(wd, wd_v, local_sem.at[5]),
    ]
    for load in loads:
        load.start()

    lane = lax.broadcasted_iota(jnp.int32, (8, 128), 1)
    mine = (lane >> 6) == c
    idf, prf = ids[...].astype(F32), prob[...].astype(F32)
    route[c, 0:8, :] = jnp.where(mine, jnp.concatenate([idf, idf], axis=1), 0.0)
    route[c, 8:16, :] = jnp.where(mine, jnp.concatenate([prf, prf], axis=1), 0.0)

    pl.semaphore_wait(barrier, TPS - 1 + 1 + 4)

    h = tokens // 2

    def exchange_of(p):
        start, size = PARTS[p]
        at = pl.ds(start, size)
        return [
            remote(attn.at[0:h, quarter(far, start, size)], af.at[0, :, at], a_send.at[p, 0], a_recv.at[p, 0], me, right),
            remote(attn.at[h:tokens, quarter(far, start, size)], af.at[1, :, at], a_send.at[p, 1], a_recv.at[p, 1], me, left),
            remote(attn.at[:, quarter(right, start, size)], ar.at[0, :, at], a_send.at[p, 2], a_recv.at[p, 2], me, right),
            remote(attn.at[:, quarter(left, start, size)], ar.at[1, :, at], a_send.at[p, 3], a_recv.at[p, 3], me, left),
            remote(af.at[0, :, at], ar.at[2, 0:h, at], a_send.at[p, 4], a_recv.at[p, 4], me, right),
            remote(af.at[1, :, at], ar.at[2, h:tokens, at], a_send.at[p, 5], a_recv.at[p, 5], me, left),
        ]

    exchange = [exchange_of(p) for p in range(2)]

    def onward(p):
        for i in range(2):
            exchange[p][i].wait_recv()
            exchange[p][4 + i].start()

    for e in exchange[0][:4]:
        e.start()
    routes = remote(route.at[c], route.at[c], route_sem.at[0], route_sem.at[1], mate, t)
    routes.start()
    for k in (1, NZ - 1):
        tell(known.at[0], along_z(k), t)
    for k in (1, NY - 1):
        tell(known.at[0], along_y(k), t)
    onward(0)
    for e in exchange[1][:4]:
        e.start()
    pl.semaphore_wait(known.at[0], 4)
    for k in (2, NZ - 2):
        tell(known.at[1], along_z(k), t)

    routes.wait_recv()
    both = route[0] + route[1]
    j = lax.broadcasted_iota(jnp.int32, (ROWS, 128), 0)
    tok = lax.broadcasted_iota(jnp.int32, (ROWS, 128), 1)
    d, slot = j >> 3, j & 3
    m, dy = d >> 2, d & 3
    dz = jnp.where((m & 1) == 1, (m + 1) >> 1, (NZ - (m >> 1)) & (NZ - 1))
    expert = ((((z + dz) & (NZ - 1)) * NY + ((y + dy) & (NY - 1))) * 2 + c).astype(F32)
    weight = jnp.zeros((ROWS, 128), F32)
    match = jnp.zeros((ROWS, 128), F32)
    for k in range(8):
        hit = both[k:k + 1, :] == expert
        match = jnp.where(hit, 1.0, match)
        weight = jnp.where(hit, both[8 + k:9 + k, :], weight)
    a, b = lax.broadcasted_iota(jnp.int32, (128, 128), 0), lax.broadcasted_iota(jnp.int32, (128, 128), 1)
    earlier = jnp.where((a < b) & ((a >> 6) == (b >> 6)), 1.0, 0.0).astype(BF16)
    before = jnp.dot(match.astype(BF16), earlier, preferred_element_type=F32)
    placed = jnp.where((before == slot.astype(F32)) & (((j >> 2) & 1) == (tok >> 6)), match, 0.0)
    select[...] = placed.astype(BF16)
    weighted = placed * weight
    for k in range(CHUNKS):
        combine[k] = jnp.transpose(weighted[k * CROWS:(k + 1) * CROWS, :]).astype(BF16)

    pl.semaphore_wait(known.at[1], 2)
    for k in range(1, NY):
        tell(known.at[2], along_y(k), t)

    here = pl.ds(pl.multiple_of(c * tokens, tokens), tokens)
    there = pl.ds(pl.multiple_of((1 - c) * tokens, tokens), tokens)
    tile = 256

    def attend(p, squares):
        start, size = PARTS[p]
        for i in range(2, 6):
            exchange[p][i].wait_recv()
        for i in range(start // tile, (start + size) // tile):
            s = slice(i * tile, (i + 1) * tile)
            v = hid_v[:, s].astype(F32)
            for q in range(4):
                v = v + ar[q, :, s].astype(F32)
            res[:, s] = v
            nb[here, s] = (v * gain_v[:, s]).astype(BF16)
            squares = squares + v * v
        return squares

    def swap_of(p):
        start, size = PARTS[p]
        at = pl.ds(start, size + p * EXTRA)
        return remote(nb.at[here, at], nb.at[here, at], nb_sem.at[p, 0], nb_sem.at[p, 1], mate, t)

    def place(m):
        return (m + 1) // 2 if m % 2 else (NZ - m // 2) % NZ

    def hops(k, act_on):
        for m in (2 * k, 2 * k + 1):
            def one(dy, carry, m=m):
                act_on(m, dy)
                return carry

            lax.fori_loop(1 if m == 0 else 0, NY, one, 0)

    def outward(p, m, dy):
        start, size = PARTS[p]
        d = m * NY + dy
        at = pl.ds(start, size + p * EXTRA)
        dp = (lax.rem(z + place(m), NZ) * NY + lax.rem(y + dy, NY)) * 2 + c
        return remote(og.at[block(d), at], rows.at[0, block(d), at], d_send.at[p, d], d_recv.at[p, d], dp, t)

    def keep_of(p):
        start, size = PARTS[p]
        at = pl.ds(start, size + p * EXTRA)
        return pltpu.make_async_copy(og.at[0:BLOCK, at], rows.at[0, 0:BLOCK, at], keep_sem.at[p])

    def dispatch(p, order):
        start, size = PARTS[p]
        at = slice(start, start + size + p * EXTRA)
        for k in order:
            r = slice(k * CROWS, (k + 1) * CROWS)
            og[r, at] = jnp.dot(select[r, :], nb[:, at], preferred_element_type=F32).astype(BF16)
            if k == 0:
                keep_of(p).start()
            hops(k, lambda m, dy: outward(p, m, dy).start())

    def gather_of(p, k):
        start, size = PARTS[p]
        at = pl.ds(start, size)
        r = pl.ds(k * CROWS, CROWS)
        lo, hi = pl.ds(k * CROWS, HALF), pl.ds(k * CROWS + HALF, HALF)
        snd, rcv = [g_send.at[p, k, i] for i in range(4)], [g_recv.at[p, k, i] for i in range(4)]
        return [
            remote(rows.at[0, r, at], rows.at[1, r, at], snd[0], rcv[0], me, right),
            remote(rows.at[0, r, at], rows.at[3, r, at], snd[1], rcv[1], me, left),
            remote(rows.at[1, lo, at], rows.at[2, lo, at], snd[2], rcv[2], me, right),
            remote(rows.at[3, hi, at], rows.at[2, hi, at], snd[3], rcv[3], me, left),
        ]

    gathers = [[gather_of(p, k) for k in range(CHUNKS)] for p in range(2)]

    def fetch(p, k):
        if k == 0:
            keep_of(p).wait()
        hops(k, lambda m, dy: outward(p, m, dy).wait_recv())
        gathers[p][k][0].start()
        gathers[p][k][1].start()

    def pass_on(p, k):
        gathers[p][k][0].wait_recv()
        gathers[p][k][2].start()
        gathers[p][k][1].wait_recv()
        gathers[p][k][3].start()

    def factor(r):
        return jnp.sum(rows[0, r, cols:cols + EXTRA].astype(F32), axis=1, keepdims=True)

    def hidden_rows(p, k):
        start, size = PARTS[p]
        r = slice(k * CROWS, (k + 1) * CROWS)
        if p == 0:
            g = jnp.zeros((CROWS, wg_v.shape[1]), F32)
            u = jnp.zeros((CROWS, wu_v.shape[1]), F32)
        else:
            g, u = g_acc[r, :], u_acc[r, :]
        for q, src in ((0, t), (1, left), (2, far), (3, right)):
            w = pl.ds(pl.multiple_of(src * cols + start, 256), size)
            x = rows[q, r, start:start + size]
            g = g + jnp.dot(x, wg_v[w, :], preferred_element_type=F32)
            u = u + jnp.dot(x, wu_v[w, :], preferred_element_type=F32)
        if p == 0:
            g_acc[r, :] = g
            u_acc[r, :] = u
        else:
            f = factor(r)
            g, u = g * f, u * f
            v = (g / (1.0 + jnp.exp(-g)) * u).astype(BF16)
            act[r, :] = v
            v = jnp.abs(v.astype(F32))
            peak[...] = jnp.maximum(peak[...], jnp.max(v.reshape(CROWS // 8, 8, v.shape[1]), axis=0))

    def down(k):
        r = slice(k * CROWS, (k + 1) * CROWS)
        x = act[r, :]
        for i, dst in ((1, far), (0, right), (2, left)):
            pb[i, r, :] = jnp.dot(x, wd_v[:, quarter(dst)], preferred_element_type=F32).astype(BF16)
        own[r, :] = jnp.dot(x, wd_v[:, quarter(t)], preferred_element_type=F32)

    def reduce_of(k):
        r0 = k * CROWS
        lo, hi = pl.ds(r0, HALF), pl.ds(r0 + HALF, HALF)
        f = pl.ds(k * HALF, HALF)
        snd, rcv = [r_send.at[k, i] for i in range(6)], [r_recv.at[k, i] for i in range(6)]
        return [
            remote(pb.at[1, lo], rf.at[0, f], snd[0], rcv[0], me, right),
            remote(pb.at[1, hi], rf.at[1, f], snd[1], rcv[1], me, left),
            remote(pb.at[0, hi], rs.at[0, hi], snd[2], rcv[2], me, right),
            remote(pb.at[2, lo], rs.at[1, lo], snd[3], rcv[3], me, left),
            remote(fs.at[0, f], rs.at[0, lo], snd[4], rcv[4], me, right),
            remote(fs.at[1, f], rs.at[1, hi], snd[5], rcv[5], me, left),
        ]

    reduces = [reduce_of(k) for k in range(CHUNKS)]

    def finish(p, k):
        gathers[p][k][2].wait_recv()
        gathers[p][k][3].wait_recv()
        hidden_rows(p, k)
        if p == 1:
            down(k)
            for i in range(4):
                reduces[k][i].start()

    def second_hop(k):
        r0 = k * CROWS
        f = slice(k * HALF, (k + 1) * HALF)
        reduces[k][0].wait_recv()
        fs[0, f] = (rf[0, f].astype(F32) + pb[0, r0:r0 + HALF].astype(F32)).astype(BF16)
        reduces[k][4].start()
        reduces[k][1].wait_recv()
        fs[1, f] = (rf[1, f].astype(F32) + pb[2, r0 + HALF:r0 + CROWS].astype(F32)).astype(BF16)
        reduces[k][5].start()

    def homeward(m, dy):
        d = m * NY + dy
        dp = (lax.rem(z + NZ - place(m), NZ) * NY + lax.rem(y + NY - dy, NY)) * 2 + c
        return remote(oq.at[block(d)], back.at[block(d)], b_send.at[d], b_recv.at[d], dp, t)

    stay = pltpu.make_async_copy(oq.at[0:BLOCK], back.at[0:BLOCK], keep_sem.at[2])

    def send_back(k):
        r = slice(k * CROWS, (k + 1) * CROWS)
        for i in range(2, 6):
            reduces[k][i].wait_recv()
        oq[r, :] = (own[r, :] + rs[0, r].astype(F32) + rs[1, r].astype(F32)).astype(BF16)
        if k == 0:
            stay.start()
        hops(k, lambda m, dy: homeward(m, dy).start())

    def collect(k):
        r = slice(k * CROWS, (k + 1) * CROWS)
        if k == 0:
            stay.wait()
        hops(k, lambda m, dy: homeward(m, dy).wait_recv())
        got = jnp.dot(combine[k, there, :], back[r, :], preferred_element_type=F32)
        mo[...] = got if k == LAST[0] else mo[...] + got
        if k == LAST[-1]:
            give.start()
        res[...] = res[...] + jnp.dot(combine[k, here, :], back[r, :], preferred_element_type=F32)

    give = remote(mo, mr, m_sem.at[0], m_sem.at[1], mate, t)

    for i in range(3):
        loads[i].wait()
    squares = attend(0, jnp.zeros((tokens, tile), F32))
    swaps = [swap_of(p) for p in range(2)]
    swaps[0].start()
    onward(1)
    pl.semaphore_wait(known.at[2], NY - 1)
    swaps[0].wait_recv()
    dispatch(0, FIRST)
    squares = attend(1, squares)
    sq[0] = jnp.broadcast_to(jnp.sum(squares, axis=1, keepdims=True), (tokens, 128))
    share = [
        remote(sq.at[0], sq.at[r], sq_send.at[r - 1], sq_recv.at[r - 1], me, lax.rem(t + r, TPS))
        for r in range(1, TPS)
    ]
    for s in share:
        s.start()
    fetch(0, FIRST[0])
    for s in share:
        s.wait_recv()
    inv = lax.rsqrt((sq[0] + sq[1] + sq[2] + sq[3]) / width + EPS)
    high = inv.astype(BF16).astype(F32)
    middle = (inv - high).astype(BF16).astype(F32)
    at = lax.broadcasted_iota(jnp.int32, (tokens, EXTRA), 1)
    terms = jnp.where(at == 0, high, jnp.where(at == 1, middle, jnp.where(at == 2, inv - high - middle, 0.0)))
    nb[here, cols:cols + EXTRA] = terms.astype(BF16)
    swaps[1].start()
    fetch(0, FIRST[1])
    pass_on(0, FIRST[0])
    swaps[1].wait_recv()
    dispatch(1, LAST)
    peak[...] = jnp.zeros(peak.shape, F32)

    units = [(0, k) for k in FIRST] + [(1, k) for k in LAST]
    n = len(units)
    for i in range(2, n + 4):
        if i < n:
            fetch(*units[i])
        if i - 1 < n:
            pass_on(*units[i - 1])
        if i == 2:
            for load in loads[3:]:
                load.wait()
        if i - 3 >= CHUNKS and i - 3 < n:
            second_hop(units[i - 3][1])
        if i - 2 < n:
            finish(*units[i - 2])
        if i == n + 1:
            hm[0] = jnp.broadcast_to(jnp.max(peak[...]), (8, 128))
            tops = [
                remote(hm.at[0], hm.at[r], h_send.at[r - 1], h_recv.at[r - 1], me, lax.rem(t + r, TPS))
                for r in range(1, TPS)
            ]
            for s in tops:
                s.start()
        if i == n + 1:
            largest = jnp.zeros((CROWS, 1), F32)
            for k in range(CHUNKS):
                r = slice(k * CROWS, (k + 1) * CROWS)
                top = jnp.zeros((CROWS, 128), F32)
                for q in range(4):
                    for l in range(cols // 128):
                        top = jnp.maximum(top, jnp.abs(rows[q, r, l * 128:(l + 1) * 128].astype(F32)))
                largest = jnp.maximum(largest, jnp.max(top, axis=1, keepdims=True) * factor(r))
            amax_in[0] = jnp.max(largest)
        if i - 4 >= CHUNKS:
            send_back(units[i - 4][1])
        if i == n + 2:
            for s in tops:
                s.wait_recv()
            amax_hid[0] = jnp.max(jnp.maximum(jnp.maximum(hm[0], hm[1]), jnp.maximum(hm[2], hm[3])))
            collect(LAST[0])
    for k in LAST[1:]:
        collect(k)
    give.wait_recv()
    out[...] = (res[...] + mr[...]).astype(BF16)

    for s in (*exchange[0], *exchange[1], routes, *share, *swaps, *tops, give):
        s.wait_send()
    for k in range(CHUNKS):
        for s in (*gathers[0][k], *gathers[1][k], *reduces[k]):
            s.wait_send()

        def drain(m, dy):
            outward(0, m, dy).wait_send()
            outward(1, m, dy).wait_send()
            homeward(m, dy).wait_send()

        hops(k, drain)


def on_device(attn_partial, hidden_in, norm_gain, expert_ids, route_prob, w_gate, w_up, w_down):
    tokens, cols = hidden_in.shape
    width, ff = w_gate.shape[1:]
    vmem, anywhere = pl.BlockSpec(memory_space=pltpu.VMEM), pl.BlockSpec(memory_space=pl.ANY)
    smem = pl.BlockSpec(memory_space=pltpu.SMEM)
    dma = pltpu.SemaphoreType.DMA
    V = pltpu.VMEM
    scratch = [
        V((tokens, cols), BF16), V((1, cols), F32), V((width, ff), BF16), V((width, ff), BF16), V((ff, width), BF16), dma((6,)),
        pltpu.SemaphoreType.REGULAR((3,)),
        V((2, 16, 128), F32), dma((2,)),
        V((4, tokens, cols), BF16), V((2, tokens // 2, cols), BF16), dma((2, 6)), dma((2, 6)),
        V((tokens, cols), F32), V((4, tokens, 128), F32), dma((3,)), dma((3,)),
        V((2 * tokens, cols + EXTRA), BF16), dma((2, 2)), V((ROWS, 128), BF16), V((CHUNKS, 128, CROWS), BF16),
        V((ROWS, cols + EXTRA), BF16), V((4, ROWS, cols + EXTRA), BF16), dma((2, CHIPS)), dma((2, CHIPS)), dma((3,)),
        dma((2, CHUNKS, 4)), dma((2, CHUNKS, 4)),
        V((ROWS, ff), F32), V((ROWS, ff), F32),
        V((ROWS, ff), BF16), V((ROWS, cols), F32), V((3, ROWS, cols), BF16), V((2, ROWS // 2, cols), BF16),
        V((2, ROWS, cols), BF16), V((2, ROWS // 2, cols), BF16), dma((CHUNKS, 6)), dma((CHUNKS, 6)),
        V((ROWS, cols), BF16), V((ROWS, cols), BF16), dma((CHIPS,)), dma((CHIPS,)),
        V((tokens, cols), F32), V((tokens, cols), F32), dma((2,)),
        V((4, 8, 128), F32), dma((3,)), dma((3,)), V((8, 256), F32),
    ]
    return pl.pallas_call(
        body,
        out_shape=(
            jax.ShapeDtypeStruct((tokens, cols), BF16),
            jax.ShapeDtypeStruct((1,), F32),
            jax.ShapeDtypeStruct((1,), F32),
        ),
        in_specs=[vmem, vmem] + [anywhere] * 6,
        out_specs=(vmem, smem, smem),
        scratch_shapes=scratch,
        compiler_params=pltpu.CompilerParams(
            collective_id=0, has_side_effects=True, vmem_limit_bytes=56 << 20
        ),
    )(
        expert_ids.T, route_prob.T, attn_partial[0], hidden_in, norm_gain[None],
        w_gate[0], w_up[0], w_down[0],
    )


def solution(mesh):
    placed = (
        P("tp", "dp", None),
        P("dp", "tp"),
        P(),
        P("dp", None),
        P("dp", None),
        P("dp", None, "tp"),
        P("dp", None, "tp"),
        P("dp", "tp", None),
    )
    return jax.shard_map(
        on_device,
        mesh=mesh,
        in_specs=placed,
        out_specs=(P("dp", "tp"), P("dp"), P("dp")),
        check_vma=False,
    )
```

```python
import jax
import jax.numpy as jnp
from jax import lax
from jax.experimental import pallas as pl
from jax.experimental.pallas import tpu as pltpu
from jax.sharding import PartitionSpec as P

MESH = pl.DeviceIdType.MESH
SLOTS = 4
EPS = 1e-06
NZ, NY, TPS = 8, 4, 4
CHIPS = NZ * NY
BLOCK = 2 * SLOTS
ROWS = CHIPS * BLOCK
NEAR = NY * BLOCK
STEPS = (
    ((0, 1), (2, 3), (4, 5), (6, 7)),
    ((0,), (1, 2), (3, 4), (5, 6), (7,)),
)
CHUNKS = len(STEPS[1])
F32, BF16 = jnp.float32, jnp.bfloat16
PARTS = ((0, 768), (768, 1024))
EXTRA = 128
FIRST, LAST = (0, 1, 2, 3), (3, 4, 2, 1, 0)


def span(k, p=1):
    return STEPS[p][k][0] * NEAR, len(STEPS[p][k]) * NEAR


def body(
    ids, prob, attn, hidden, gain, wg, wu, wd,
    out, amax_in, amax_hid,
    hid_v, gain_v, wg_v, wu_v, wd_v, local_sem, known,
    route, route_sem,
    ar, a_send, a_recv,
    res, sq, sq_send, sq_recv,
    nb, nb_sem, select, combine,
    og, rows, d_send, d_recv, keep_sem,
    g_send, g_recv,
    g_acc, u_acc, act, own, pb, rf, rs, fs, r_send, r_recv,
    oq, back, near, b_send, b_recv, n_send, n_recv,
    mo, mr, m_sem,
    hm, h_send, h_recv, peak,
):
    me, t = lax.axis_index("dp"), lax.axis_index("tp")
    c, chip = lax.rem(me, 2), lax.div(me, 2)
    z, y = lax.div(chip, NY), lax.rem(chip, NY)
    tokens, width = attn.shape
    cols = width // TPS
    right, left, far = lax.rem(t + 1, TPS), lax.rem(t + 3, TPS), lax.rem(t + 2, TPS)
    mate = chip * 2 + 1 - c

    def along_z(k):
        return (lax.rem(z + k, NZ) * NY + y) * 2 + c

    def along_y(k):
        return (z * NY + lax.rem(y + k, NY)) * 2 + c

    def remote(src, dst, ssem, rsem, dp, tp):
        return pltpu.make_async_remote_copy(
            src_ref=src, dst_ref=dst, send_sem=ssem, recv_sem=rsem,
            device_id=(dp, tp), device_id_type=MESH,
        )

    def tell(sem, dp, tp):
        pl.semaphore_signal(sem, inc=1, device_id=(dp, tp), device_id_type=MESH)

    def quarter(q, start=0, size=None):
        return pl.ds(pl.multiple_of(q * cols + start, 128), cols if size is None else size)

    def block(d):
        return pl.ds(pl.multiple_of(d * BLOCK, BLOCK), BLOCK)

    barrier = pltpu.get_barrier_semaphore()
    for r in range(1, TPS):
        tell(barrier, me, lax.rem(t + r, TPS))
    tell(barrier, mate, t)
    for k in (1, NZ - 1):
        tell(barrier, along_z(k), t)
    for k in (1, NY - 1):
        tell(barrier, along_y(k), t)

    loads = [
        pltpu.make_async_copy(attn.at[:, quarter(t)], ar.at[3], local_sem.at[0]),
        pltpu.make_async_copy(hidden, hid_v, local_sem.at[1]),
        pltpu.make_async_copy(gain.at[:, quarter(t)], gain_v, local_sem.at[2]),
        pltpu.make_async_copy(wg, wg_v, local_sem.at[3]),
        pltpu.make_async_copy(wu, wu_v, local_sem.at[4]),
        pltpu.make_async_copy(wd, wd_v, local_sem.at[5]),
    ]
    for load in loads:
        load.start()

    lane = lax.broadcasted_iota(jnp.int32, (8, 128), 1)
    mine = (lane >> 6) == c
    idf, prf = ids[...].astype(F32), prob[...].astype(F32)
    route[c, 0:8, :] = jnp.where(mine, jnp.concatenate([idf, idf], axis=1), 0.0)
    route[c, 8:16, :] = jnp.where(mine, jnp.concatenate([prf, prf], axis=1), 0.0)

    pl.semaphore_wait(barrier, TPS - 1 + 1 + 4)

    def exchange_of(p):
        start, size = PARTS[p]
        at = pl.ds(start, size)
        return [
            remote(attn.at[:, quarter(to, start, size)], ar.at[i, :, at], a_send.at[p, i], a_recv.at[p, i], me, to)
            for i, to in ((2, far), (0, right), (1, left))
        ]

    exchange = [exchange_of(p) for p in range(2)]
    for e in exchange[0]:
        e.start()
    routes = remote(route.at[c], route.at[c], route_sem.at[0], route_sem.at[1], mate, t)
    routes.start()
    for k in (1, NZ - 1):
        tell(known.at[0], along_z(k), t)
    for k in (1, NY - 1):
        tell(known.at[0], along_y(k), t)
    for e in exchange[1]:
        e.start()
    pl.semaphore_wait(known.at[0], 4)
    for k in (2, NZ - 2):
        tell(known.at[1], along_z(k), t)

    routes.wait_recv()
    both = route[0] + route[1]
    j = lax.broadcasted_iota(jnp.int32, (ROWS + NEAR, 128), 0)
    tok = lax.broadcasted_iota(jnp.int32, (ROWS + NEAR, 128), 1)
    d, slot = (j >> 3) & (CHIPS - 1), j & 3
    core = jnp.where(j < ROWS, c, 1 - c)
    m, dy = d >> 2, d & 3
    dz = jnp.where((m & 1) == 1, (m + 1) >> 1, (NZ - (m >> 1)) & (NZ - 1))
    expert = ((((z + dz) & (NZ - 1)) * NY + ((y + dy) & (NY - 1))) * 2 + core).astype(F32)
    weight = jnp.zeros((ROWS + NEAR, 128), F32)
    match = jnp.zeros((ROWS + NEAR, 128), F32)
    for k in range(8):
        hit = both[k:k + 1, :] == expert
        match = jnp.where(hit, 1.0, match)
        weight = jnp.where(hit, both[8 + k:9 + k, :], weight)
    a, b = lax.broadcasted_iota(jnp.int32, (128, 128), 0), lax.broadcasted_iota(jnp.int32, (128, 128), 1)
    earlier = jnp.where((a < b) & ((a >> 6) == (b >> 6)), 1.0, 0.0).astype(BF16)
    before = jnp.dot(match.astype(BF16), earlier, preferred_element_type=F32)
    placed = jnp.where((before == slot.astype(F32)) & (((j >> 2) & 1) == (tok >> 6)), match, 0.0)
    select[...] = placed[0:ROWS].astype(BF16)
    weighted = placed * weight
    for k, (r0, n) in enumerate([span(k) for k in range(CHUNKS)] + [(ROWS, NEAR)]):
        combine[k, :, 0:n] = jnp.transpose(weighted[r0:r0 + n, :]).astype(BF16)

    pl.semaphore_wait(known.at[1], 2)
    for k in range(1, NY):
        tell(known.at[2], along_y(k), t)

    here = pl.ds(pl.multiple_of(c * tokens, tokens), tokens)
    there = pl.ds(pl.multiple_of((1 - c) * tokens, tokens), tokens)
    tile = 256

    def attend(p, squares):
        start, size = PARTS[p]
        for e in exchange[p]:
            e.wait_recv()
        for i in range(start // tile, (start + size) // tile):
            s = slice(i * tile, (i + 1) * tile)
            v = hid_v[:, s].astype(F32)
            for q in range(4):
                v = v + ar[q, :, s].astype(F32)
            res[:, s] = v
            nb[here, s] = (v * gain_v[:, s]).astype(BF16)
            squares = squares + v * v
        return squares

    def swap_of(p):
        start, size = PARTS[p]
        at = pl.ds(start, size)
        return remote(nb.at[here, at], nb.at[here, at], nb_sem.at[p, 0], nb_sem.at[p, 1], mate, t)

    def place(m):
        return (m + 1) // 2 if m % 2 else (NZ - m // 2) % NZ

    def hops(k, act_on, p=1):
        for m in STEPS[p][k]:
            def one(dy, carry, m=m):
                act_on(m, dy)
                return carry

            lax.fori_loop(1 if m == 0 else 0, NY, one, 0)

    def outward(p, m, dy):
        start, size = PARTS[p]
        d = m * NY + dy
        at = pl.ds(start, size + p * EXTRA)
        dp = (lax.rem(z + place(m), NZ) * NY + lax.rem(y + dy, NY)) * 2 + c
        return remote(og.at[block(d), at], rows.at[0, block(d), at], d_send.at[p, d], d_recv.at[p, d], dp, t)

    def keep_of(p):
        start, size = PARTS[p]
        at = pl.ds(start, size + p * EXTRA)
        return pltpu.make_async_copy(og.at[0:BLOCK, at], rows.at[0, 0:BLOCK, at], keep_sem.at[p])

    def dispatch(p, order):
        start, size = PARTS[p]
        at = slice(start, start + size + p * EXTRA)
        for k in order:
            r0, n = span(k, p)
            r = slice(r0, r0 + n)
            og[r, at] = jnp.dot(select[r, :], nb[:, at], preferred_element_type=F32).astype(BF16)
            if k == 0:
                keep_of(p).start()
            hops(k, lambda m, dy: outward(p, m, dy).start(), p)

    def gather_of(p, k):
        start, size = PARTS[p]
        at = pl.ds(start, size)
        r0, n = span(k, p)
        r, lo, hi = pl.ds(r0, n), pl.ds(r0, n // 2), pl.ds(r0 + n // 2, n // 2)
        snd, rcv = [g_send.at[p, k, i] for i in range(4)], [g_recv.at[p, k, i] for i in range(4)]
        return [
            remote(rows.at[0, r, at], rows.at[1, r, at], snd[0], rcv[0], me, right),
            remote(rows.at[0, r, at], rows.at[3, r, at], snd[1], rcv[1], me, left),
            remote(rows.at[1, lo, at], rows.at[2, lo, at], snd[2], rcv[2], me, right),
            remote(rows.at[3, hi, at], rows.at[2, hi, at], snd[3], rcv[3], me, left),
        ]

    gathers = [[gather_of(p, k) for k in range(len(STEPS[p]))] for p in range(2)]

    def fetch(p, k):
        if k == 0:
            keep_of(p).wait()
        hops(k, lambda m, dy: outward(p, m, dy).wait_recv(), p)
        gathers[p][k][0].start()
        gathers[p][k][1].start()

    def pass_on(p, k):
        gathers[p][k][0].wait_recv()
        gathers[p][k][2].start()
        gathers[p][k][1].wait_recv()
        gathers[p][k][3].start()

    def factor(r):
        return jnp.sum(rows[0, r, cols:cols + EXTRA].astype(F32), axis=1, keepdims=True)

    def hidden_rows(p, k):
        start, size = PARTS[p]
        r0, n = span(k, p)
        r = slice(r0, r0 + n)
        if p == 0:
            g = jnp.zeros((n, wg_v.shape[1]), F32)
            u = jnp.zeros((n, wu_v.shape[1]), F32)
        else:
            g, u = g_acc[r, :], u_acc[r, :]
        for q, src in ((0, t), (1, left), (2, far), (3, right)):
            w = pl.ds(pl.multiple_of(src * cols + start, 256), size)
            x = rows[q, r, start:start + size]
            g = g + jnp.dot(x, wg_v[w, :], preferred_element_type=F32)
            u = u + jnp.dot(x, wu_v[w, :], preferred_element_type=F32)
        if p == 0:
            g_acc[r, :] = g
            u_acc[r, :] = u
        else:
            f = factor(r)
            g, u = g * f, u * f
            v = (g / (1.0 + jnp.exp(-g)) * u).astype(BF16)
            act[r, :] = v
            v = jnp.abs(v.astype(F32))
            peak[...] = jnp.maximum(peak[...], jnp.max(v.reshape(n // 8, 8, v.shape[1]), axis=0))

    def down(k):
        r0, n = span(k)
        r = slice(r0, r0 + n)
        x = act[r, :]
        for i, dst in ((1, far), (0, right), (2, left)):
            pb[i, r, :] = jnp.dot(x, wd_v[:, quarter(dst)], preferred_element_type=F32).astype(BF16)
        own[r, :] = jnp.dot(x, wd_v[:, quarter(t)], preferred_element_type=F32)

    def reduce_of(k):
        r0, n = span(k)
        lo, hi, f = pl.ds(r0, n // 2), pl.ds(r0 + n // 2, n // 2), pl.ds(r0 // 2, n // 2)
        snd, rcv = [r_send.at[k, i] for i in range(6)], [r_recv.at[k, i] for i in range(6)]
        return [
            remote(pb.at[1, lo], rf.at[0, f], snd[0], rcv[0], me, right),
            remote(pb.at[1, hi], rf.at[1, f], snd[1], rcv[1], me, left),
            remote(pb.at[0, hi], rs.at[0, hi], snd[2], rcv[2], me, right),
            remote(pb.at[2, lo], rs.at[1, lo], snd[3], rcv[3], me, left),
            remote(fs.at[0, f], rs.at[0, lo], snd[4], rcv[4], me, right),
            remote(fs.at[1, f], rs.at[1, hi], snd[5], rcv[5], me, left),
        ]

    reduces = [reduce_of(k) for k in range(CHUNKS)]

    def finish(p, k):
        gathers[p][k][2].wait_recv()
        gathers[p][k][3].wait_recv()
        hidden_rows(p, k)
        if p == 1:
            down(k)
            for i in range(4):
                reduces[k][i].start()

    def second_hop(k):
        r0, n = span(k)
        f = slice(r0 // 2, (r0 + n) // 2)
        reduces[k][0].wait_recv()
        fs[0, f] = (rf[0, f].astype(F32) + pb[0, r0:r0 + n // 2].astype(F32)).astype(BF16)
        reduces[k][4].start()
        reduces[k][1].wait_recv()
        fs[1, f] = (rf[1, f].astype(F32) + pb[2, r0 + n // 2:r0 + n].astype(F32)).astype(BF16)
        reduces[k][5].start()

    def homeward(m, dy):
        d = m * NY + dy
        dp = (lax.rem(z + NZ - place(m), NZ) * NY + lax.rem(y + NY - dy, NY)) * 2 + c
        return remote(oq.at[block(d)], back.at[block(d)], b_send.at[d], b_recv.at[d], dp, t)

    stay = pltpu.make_async_copy(oq.at[0:BLOCK], back.at[0:BLOCK], keep_sem.at[2])

    def across(dy):
        dp = (z * NY + lax.rem(y + NY - dy, NY)) * 2 + 1 - c
        return remote(oq.at[block(dy)], near.at[block(dy)], n_send.at[dy], n_recv.at[dy], dp, t)

    def send_back(k):
        r0, n = span(k)
        r = slice(r0, r0 + n)
        for i in range(2, 6):
            reduces[k][i].wait_recv()
        oq[r, :] = (own[r, :] + rs[0, r].astype(F32) + rs[1, r].astype(F32)).astype(BF16)
        if k == 0:
            for dy in range(NY):
                across(dy).start()
            stay.start()
        hops(k, lambda m, dy: homeward(m, dy).start())

    def collect(k):
        r0, n = span(k)
        r = slice(r0, r0 + n)
        hops(k, lambda m, dy: homeward(m, dy).wait_recv())
        if k:
            got = jnp.dot(combine[k, there, 0:n], back[r, :], preferred_element_type=F32)
            mo[...] = got if k == LAST[0] else mo[...] + got
            if k == LAST[-2]:
                give.start()
            res[...] = res[...] + jnp.dot(combine[k, here, 0:n], back[r, :], preferred_element_type=F32)
            return
        stay.wait()
        for dy in range(NY):
            across(dy).wait_recv()
        last = jnp.dot(combine[0, here, 0:n], back[r, :], preferred_element_type=F32)
        last = last + jnp.dot(combine[CHUNKS, here, 0:n], near[...], preferred_element_type=F32)
        out[...] = (res[...] + last).astype(BF16)

    give = remote(mo, mr, m_sem.at[0], m_sem.at[1], mate, t)

    for i in range(3):
        loads[i].wait()
    squares = attend(0, jnp.zeros((tokens, tile), F32))
    swaps = [swap_of(p) for p in range(2)]
    swaps[0].start()
    pl.semaphore_wait(known.at[2], NY - 1)
    swaps[0].wait_recv()
    dispatch(0, FIRST)
    units = [(0, k) for k in FIRST] + [(1, k) for k in LAST]
    squares = attend(1, squares)
    swaps[1].start()
    total = jnp.sum(squares, axis=1, keepdims=True)
    total = jnp.transpose(jnp.broadcast_to(total, (tokens, 128)))[0:8, :]
    sq[0] = jnp.where(mine, jnp.concatenate([total, total], axis=1), 0.0)
    share = [
        remote(sq.at[0], sq.at[2 * r + x], sq_send.at[2 * r + x], sq_recv.at[2 * r + x],
               mate if x else me, lax.rem(t + r, TPS))
        for r in range(TPS) for x in range(2) if r or x
    ]
    for s in share:
        s.start()
    fetch(*units[0])
    for s in share:
        s.wait_recv()
    total = sq[0]
    for i in range(1, 2 * TPS):
        total = total + sq[i]
    inv = lax.rsqrt(total[0:1, :] / width + EPS)
    high = inv.astype(BF16).astype(F32)
    middle = (inv - high).astype(BF16).astype(F32)
    at = lax.broadcasted_iota(jnp.int32, (EXTRA, 128), 0)
    terms = jnp.where(at == 0, high, jnp.where(at == 1, middle, jnp.where(at == 2, inv - high - middle, 0.0)))
    nb[:, cols:cols + EXTRA] = jnp.transpose(terms).astype(BF16)
    swaps[1].wait_recv()
    dispatch(1, LAST[:2])
    fetch(*units[1])
    pass_on(*units[0])
    dispatch(1, LAST[2:])
    fetch(*units[2])
    pass_on(*units[1])
    peak[...] = jnp.zeros(peak.shape, F32)

    n = len(units)
    for i in range(3, n + 4):
        if i < n:
            fetch(*units[i])
        if i - 1 < n:
            pass_on(*units[i - 1])
        if i == 3:
            for load in loads[3:]:
                load.wait()
            finish(*units[0])
        if i - 3 >= len(FIRST) and i - 3 < n:
            second_hop(units[i - 3][1])
        if i - 2 < n:
            finish(*units[i - 2])
        if i == n + 1:
            hm[0] = jnp.broadcast_to(jnp.max(peak[...]), (8, 128))
            tops = [
                remote(hm.at[0], hm.at[r], h_send.at[r - 1], h_recv.at[r - 1], me, lax.rem(t + r, TPS))
                for r in range(1, TPS)
            ]
            for s in tops:
                s.start()
        if i - 4 >= len(FIRST):
            send_back(units[i - 4][1])
        if i == n + 2:
            largest = jnp.zeros((NEAR, 1), F32)
            for k in range(ROWS // NEAR):
                r = slice(k * NEAR, (k + 1) * NEAR)
                top = jnp.zeros((NEAR, 128), F32)
                for q in range(4):
                    for l in range(cols // 128):
                        top = jnp.maximum(top, jnp.abs(rows[q, r, l * 128:(l + 1) * 128].astype(F32)))
                largest = jnp.maximum(largest, jnp.max(top, axis=1, keepdims=True) * factor(r))
            amax_in[0] = jnp.max(largest)
            for s in tops:
                s.wait_recv()
            amax_hid[0] = jnp.max(jnp.maximum(jnp.maximum(hm[0], hm[1]), jnp.maximum(hm[2], hm[3])))
            for s in (*exchange[0], *exchange[1], routes, *share, *swaps):
                s.wait_send()
            for g in (*gathers[0], *gathers[1], *(reduces[k] for k in LAST[:-2])):
                for s in g:
                    s.wait_send()

            def drain(m, dy):
                outward(0, m, dy).wait_send()
                outward(1, m, dy).wait_send()

            for k in range(CHUNKS):
                hops(k, drain)
            collect(LAST[0])
            for k in LAST[:-2]:
                hops(k, lambda m, dy: homeward(m, dy).wait_send())
    for k in LAST[1:-1]:
        collect(k)
    give.wait_recv()
    res[...] = res[...] + mr[...]
    collect(LAST[-1])

    for s in (*tops, give, *reduces[LAST[-2]], *reduces[LAST[-1]]):
        s.wait_send()
    for k in LAST[-2:]:
        hops(k, lambda m, dy: homeward(m, dy).wait_send())
    for dy in range(NY):
        across(dy).wait_send()


def on_device(attn_partial, hidden_in, norm_gain, expert_ids, route_prob, w_gate, w_up, w_down):
    tokens, cols = hidden_in.shape
    width, ff = w_gate.shape[1:]
    vmem, anywhere = pl.BlockSpec(memory_space=pltpu.VMEM), pl.BlockSpec(memory_space=pl.ANY)
    smem = pl.BlockSpec(memory_space=pltpu.SMEM)
    dma = pltpu.SemaphoreType.DMA
    V = pltpu.VMEM
    scratch = [
        V((tokens, cols), BF16), V((1, cols), F32), V((width, ff), BF16), V((width, ff), BF16), V((ff, width), BF16), dma((6,)),
        pltpu.SemaphoreType.REGULAR((3,)),
        V((2, 16, 128), F32), dma((2,)),
        V((4, tokens, cols), BF16), dma((2, 3)), dma((2, 3)),
        V((tokens, cols), F32), V((2 * TPS, 8, 128), F32), dma((2 * TPS,)), dma((2 * TPS,)),
        V((2 * tokens, cols + EXTRA), BF16), dma((2, 2)), V((ROWS, 128), BF16), V((CHUNKS + 1, 128, 128), BF16),
        V((ROWS, cols + EXTRA), BF16), V((4, ROWS, cols + EXTRA), BF16), dma((2, CHIPS)), dma((2, CHIPS)), dma((3,)),
        dma((2, CHUNKS, 4)), dma((2, CHUNKS, 4)),
        V((ROWS, ff), F32), V((ROWS, ff), F32),
        V((ROWS, ff), BF16), V((ROWS, cols), F32), V((3, ROWS, cols), BF16), V((2, ROWS // 2, cols), BF16),
        V((2, ROWS, cols), BF16), V((2, ROWS // 2, cols), BF16), dma((CHUNKS, 6)), dma((CHUNKS, 6)),
        V((ROWS, cols), BF16), V((ROWS, cols), BF16), V((NEAR, cols), BF16), dma((CHIPS,)), dma((CHIPS,)), dma((NY,)), dma((NY,)),
        V((tokens, cols), F32), V((tokens, cols), F32), dma((2,)),
        V((4, 8, 128), F32), dma((3,)), dma((3,)), V((8, 256), F32),
    ]
    return pl.pallas_call(
        body,
        out_shape=(
            jax.ShapeDtypeStruct((tokens, cols), BF16),
            jax.ShapeDtypeStruct((1,), F32),
            jax.ShapeDtypeStruct((1,), F32),
        ),
        in_specs=[vmem, vmem] + [anywhere] * 6,
        out_specs=(vmem, smem, smem),
        scratch_shapes=scratch,
        compiler_params=pltpu.CompilerParams(
            collective_id=0, has_side_effects=True, vmem_limit_bytes=56 << 20
        ),
    )(
        expert_ids.T, route_prob.T, attn_partial[0], hidden_in, norm_gain[None],
        w_gate[0], w_up[0], w_down[0],
    )


def solution(mesh):
    placed = (
        P("tp", "dp", None),
        P("dp", "tp"),
        P(),
        P("dp", None),
        P("dp", None),
        P("dp", None, "tp"),
        P("dp", None, "tp"),
        P("dp", "tp", None),
    )
    return jax.shard_map(
        on_device,
        mesh=mesh,
        in_specs=placed,
        out_specs=(P("dp", "tp"), P("dp"), P("dp")),
        check_vma=False,
    )
```
